32 devices in a mesh: ob: 8 (over z, core), pt: 4 (over y, x).
Axes of the slice: x: 2, y: 2, z: 4, core: 2. Of those that a mesh axis runs over, the one named last changes fastest.
Arguments:
- orbitals: float32 [128, 262144], P(('ob', 'pt')), may hold values from -32 to 32, as said below
- potential: float32 [262144], replicated, may hold values from 0 to 2
- cutoff: float32 [1], replicated, may hold values from 0.4 to 1
- eigvec: float32 [128, 128], replicated, may hold values from -3 to 3, as said below
Outputs:
- gram: float32 [128, 128], P(('ob', 'pt'))
- hamil_sub: float32 [128, 128], P(('ob', 'pt'))
- rotated: float32 [128, 262144], P(None, ('ob', 'pt'))
- residual: float32 [128, 262144], P(None, ('ob', 'pt'))
- ritz: float32 [128], replicated
The draws below stay inside these ranges and needn't reach their ends.
Inputs may be any that keep to these rules, and one draw needn't show every extreme that they name: `orbitals`: each orbital is a rough field whose scale differs from orbital to orbital and from region to region of the grid. `eigvec`: A full-rank matrix with a unit-sized diagonal and independent off-diagonal entries.
All inputs are finite; a program needn't handle non-finite values.
Results may differ from the reference program's by a relative error of at most 0.00027.
Values sent between devices are 32-bit elements; how exact they have to be, the bound alone decides.
A program may use at most 128 MiB of HBM per device.

```python
import jax
import jax.numpy as jnp
from jax import lax

G = 64
DEGREE = 12
ORB_DEV = 4
NORB = 128
NPTS = 262144


def draw_orbitals(key, part):
    key_base = jax.random.fold_in(key, 11)
    key_scale = jax.random.fold_in(key, 13)
    key_region = jax.random.fold_in(key, 14)
    points = lax.iota(jnp.int32, NPTS)
    x_coord = points // (G * G)
    y_coord = points // G % G
    z_coord = points % G
    block_id = x_coord * 8 // G * 64 + y_coord * 8 // G * 8 + z_coord * 8 // G
    base = jnp.clip(jax.random.normal(key_base, (NORB, NPTS), jnp.float32), -4.0, 4.0)
    region_table = jnp.exp(jax.random.uniform(key_region, (512,), jnp.float32, jnp.log(0.5), jnp.log(2.0)))
    orb_scale = jnp.exp(jax.random.uniform(key_scale, (NORB, 1), jnp.float32, jnp.log(0.4), jnp.log(4.0)))
    region = region_table[block_id][None, :]
    return jnp.clip(base * orb_scale * region, -32.0, 32.0)


def draw_eigvec(key, part):
    key_off = jax.random.fold_in(key, 21)
    off_diag = jnp.clip(jax.random.normal(key_off, (NORB, NORB), jnp.float32), -4.0, 4.0)
    return jnp.eye(NORB, dtype=jnp.float32) + 0.6 * off_diag / jnp.sqrt(jnp.float32(NORB))


def setup_inputs(seed: int = 0) -> dict:
    key_of = jax.random.split(jax.random.key(seed), 5)
    orbitals = draw_orbitals(jax.random.fold_in(key_of[4], 71), 0)
    potential = jnp.clip(jax.random.uniform(key_of[1], (NPTS,), jnp.float32, 0.0, 2.0), 0.0, 2.0)
    cutoff = jnp.clip(jax.random.uniform(key_of[2], (1,), jnp.float32, 0.4, 1.0), 0.4, 1.0)
    eigvec = draw_eigvec(jax.random.fold_in(key_of[4], 71), 0)
    return dict(orbitals=orbitals, potential=potential, cutoff=cutoff, eigvec=eigvec)


upper_bound = 8.0
quot_eps = 1e-6


def apply_ham(fields, potential):
    points = fields.shape[-1]
    plane_len = G * G
    x_pair = jnp.roll(fields, plane_len, axis=-1) + jnp.roll(fields, -plane_len, axis=-1)
    cube_view = fields.reshape(fields.shape[0], G, plane_len)
    y_pair = (jnp.roll(cube_view, G, axis=-1) + jnp.roll(cube_view, -G, axis=-1)).reshape(fields.shape)
    z_index = lax.broadcasted_iota(jnp.int32, (1, points), 1) % G
    z_lower = jnp.where(z_index == 0, jnp.roll(fields, 1 - G, axis=-1), jnp.roll(fields, 1, axis=-1))
    z_upper = jnp.where(z_index == G - 1, jnp.roll(fields, G - 1, axis=-1), jnp.roll(fields, -1, axis=-1))
    return -0.5 * (x_pair + y_pair + z_lower + z_upper - 6.0 * fields) + potential * fields


def chebyshev(fields, potential, cutoff):
    center = 0.5 * (upper_bound + cutoff[0])
    half_width = 0.5 * (upper_bound - cutoff[0])
    current = (apply_ham(fields, potential) - center * fields) / half_width

    def advance(turn_idx, carry):
        previous, present = carry
        following = 2.0 * (apply_ham(present, potential) - center * present) / half_width - previous
        return (present, following)

    previous, current = lax.fori_loop(0, DEGREE - 1, advance, (fields, current))
    return current, apply_ham(current, potential)


def reference(orbitals, potential, cutoff, eigvec):
    blocks = orbitals.reshape(-1, ORB_DEV, NPTS)
    filtered, applied = lax.map(lambda block: chebyshev(block, potential, cutoff), blocks)
    filtered = filtered.reshape(NORB, NPTS)
    applied = applied.reshape(NORB, NPTS)
    high = lax.Precision.HIGHEST
    gram = jnp.dot(filtered, filtered.T, precision=high) / NPTS
    hamil_sub = jnp.dot(filtered, applied.T, precision=high) / NPTS
    rotated = jnp.dot(eigvec.T, filtered, precision=high)
    rot_applied = jnp.dot(eigvec.T, applied, precision=high)
    numer = jnp.sum(eigvec * jnp.dot(hamil_sub, eigvec, precision=high), axis=0)
    denom = jnp.sum(eigvec * jnp.dot(gram, eigvec, precision=high), axis=0)
    ritz = numer / (denom + quot_eps)
    residual = rot_applied - ritz[:, None] * rotated
    return (gram, hamil_sub, rotated, residual, ritz)
```

```python
import functools

import jax
import jax.numpy as jnp
from jax import lax
from jax.experimental import pallas as pl
from jax.experimental.pallas import tpu as pltpu
from jax.sharding import PartitionSpec as P

G = 64
DEGREE = 12
LANES = 128
SUBS = 8
ROWS = G * G // LANES
BLK = ROWS // SUBS
CHUNK = 16
MESH = pl.DeviceIdType.MESH
upper_bound = 8.0
quot_eps = 1e-06


def split(x):
    hi = x.astype(jnp.bfloat16)
    return hi, (x - hi.astype(jnp.float32)).astype(jnp.bfloat16)


def shift_matrix():
    row = lax.broadcasted_iota(jnp.int32, (2 * LANES, 2 * LANES), 0) % LANES
    col = lax.broadcasted_iota(jnp.int32, (2 * LANES, 2 * LANES), 1)
    lane = col % LANES
    step = (row - lane) % G
    z_pair = (row // G == lane // G) & ((step == 1) | (step == G - 1))
    swap = (row + G) % LANES == lane
    both = jnp.where(swap, 1.0, 0.0) + jnp.where((col < LANES) & z_pair, 1.0, 0.0)
    return both.astype(jnp.bfloat16)


def lateral(v, shifts):
    hi, lo = split(v.reshape(-1, LANES))
    both = jnp.dot(
        jnp.concatenate([hi, lo], axis=1), shifts, preferred_element_type=jnp.float32
    )
    near = both[:, :LANES].reshape(v.shape)
    w = both[:, LANES:].reshape(v.shape)
    below = jnp.concatenate([pltpu.roll(w[:, BLK - 1 :], 1, 2), w[:, : BLK - 1]], axis=1)
    above = jnp.concatenate([w[:, 1:], pltpu.roll(w[:, :1], SUBS - 1, 2)], axis=1)
    low = lax.broadcasted_iota(jnp.int32, (1, 1, 1, LANES), 3) < G
    return near + jnp.where(low, below, above)


def kernel(
    n_ob, n_pt,
    cut_ref, pot_hbm, orb_hbm, eig_ref,
    gram_out, hamil_out, ritz_out, rot_hbm, res_hbm,
    ext, spare, coef, pot, shifts, zbuf, appl, filt_all, appl_all, est, rot, rota,
    quot, quot_in, part, part_in,
    load_sem, pot_sem, zsend, zrecv, psend, precv, qsend, qrecv, gsend, grecv, out_sem,
):
    waves = ext.shape[0]
    outer, peers, n_dev = n_ob // 2, 2 * n_pt, n_ob * n_pt
    norb = eig_ref.shape[1]
    ppl = G // outer
    n_plane, _, n_sub = filt_all.shape[:3]
    per_plane = SUBS // n_sub
    npts = G * G * G
    ob, pt = lax.axis_index("ob"), lax.axis_index("pt")
    me = ob * n_pt + pt
    group = ob // 2
    seat = ob % 2 * n_pt + pt

    def device(i):
        return (i // n_pt, i % n_pt)

    half = group // max(1, outer // 2)
    mirrored = half * (outer - 1 - group) + (1 - half) * group

    def other_group(i):
        t = outer - 1 - i - (i + mirrored + 1) // outer
        return half * (outer - 1 - t) + (1 - half) * t

    barrier = pltpu.get_barrier_semaphore()

    def greet(k, c):
        pl.semaphore_signal(
            barrier, inc=1, device_id=device((me + k) % n_dev), device_id_type=MESH
        )
        return c

    def load(w, b):
        return pltpu.make_async_copy(
            orb_hbm.at[:, :, b * waves + w, :], ext.at[w, pl.ds(1, G), b], load_sem.at[w, b]
        )

    def load_pot(b):
        return pltpu.make_async_copy(pot_hbm.at[:, :, b, :], pot.at[:, b], pot_sem.at[b])

    for b in range(BLK):
        load(0, b).start()
    for b in range(BLK):
        load_pot(b).start()
    for w in range(1, waves):
        for b in range(BLK):
            load(w, b).start()
    lax.fori_loop(1, n_dev, greet, 0)

    cut = cut_ref[0]
    center = 0.5 * (upper_bound + cut)
    half_width = 0.5 * (upper_bound - cut)
    inv = 1.0 / half_width
    shifts[...] = shift_matrix()
    for w in range(waves):
        hi, lo = split(eig_ref[pl.ds(w * n_dev, n_dev), :].T)
        est[w] = jnp.concatenate([hi, lo, hi], axis=1)
    for b in range(BLK):
        load_pot(b).wait()

    def prep(x, c):
        coef[x] = (2.0 * inv) * (pot[x] + (3.0 - center))
        return c

    lax.fori_loop(0, G, prep, 0)

    def sweep(cur, dst, first):
        for q in range(G // CHUNK):
            lat = lateral(cur[pl.ds(q * CHUNK, CHUNK)], shifts[...])
            for u in range(CHUNK):
                x = q * CHUNK + u
                s = (cur[(x - 1) % G] + cur[(x + 1) % G]) + lat[u]
                g = coef[x] * cur[x] - inv * s
                dst[x] = 0.5 * g if first else g - dst[x]

    def zcopy(w, i):
        to = other_group(i)
        return pltpu.make_async_remote_copy(
            src_ref=ext.at[w, pl.ds(to * ppl, ppl + 2)],
            dst_ref=zbuf.at[group, w],
            send_sem=zsend.at[w, to],
            recv_sem=zrecv.at[w, group],
            device_id=(to * 2 + ob % 2, pt),
            device_id_type=MESH,
        )

    def zarrival(w, g):
        return pltpu.make_async_remote_copy(
            src_ref=zbuf.at[g, w],
            dst_ref=zbuf.at[g, w],
            send_sem=zsend.at[w, g],
            recv_sem=zrecv.at[w, g],
            device_id=(g * 2 + ob % 2, pt),
            device_id_type=MESH,
        )

    def piece(ref, first_plane, to):
        planes = pl.ds(first_plane + to // per_plane * n_plane, n_plane)
        if n_sub == SUBS:
            return ref.at[planes]
        return ref.at[planes, :, pl.ds(pl.multiple_of(to % per_plane * n_sub, n_sub), n_sub)]

    def dispatch(w, g, i):
        src, first = ((zbuf, 1), (appl, 0))[i]
        dst = (filt_all, appl_all)[i].at[:, :, :, w * n_dev + g * peers + seat, :]

        def send(k, c):
            to = (seat + k) % peers
            pltpu.make_async_remote_copy(
                src_ref=piece(src.at[g, w], first, to),
                dst_ref=dst,
                send_sem=psend.at[w, i],
                recv_sem=precv.at[w, i],
                device_id=(group * 2 + to // n_pt, to % n_pt),
                device_id_type=MESH,
            ).start()
            return c

        lax.fori_loop(1, peers, send, 0)
        pltpu.make_async_copy(piece(src.at[g, w], first, seat), dst, precv.at[w, i]).start()

    def process(w, g):
        dispatch(w, g, 0)
        src = zbuf.at[g, w]
        lat = lateral(src[pl.ds(1, ppl)], shifts[...])
        for x in range(ppl):
            s = (src[x] + src[x + 2]) + lat[x]
            appl[g, w, x] = (pot[group * ppl + x] + 3.0) * src[x + 1] - 0.5 * s
        dispatch(w, g, 1)

    def filter_wave(w, c):
        for b in range(BLK):
            load(w, b).wait()
        f = ext.at[w, pl.ds(1, G)]
        sweep(f, spare, True)

        def pair(j, c):
            sweep(spare, f, False)
            sweep(f, spare, False)
            return c

        lax.fori_loop(0, (DEGREE - 2) // 2, pair, 0)
        sweep(spare, f, False)
        ext[w, 0] = ext[w, G]
        ext[w, G + 1] = ext[w, 1]

        @pl.when(w == 0)
        def _():
            pl.semaphore_wait(barrier, n_dev - 1)

        for i in range(outer - 1):
            zcopy(w, i).start()
        zbuf[group, w] = ext[w, pl.ds(group * ppl, ppl + 2)]
        process(w, group)
        return c

    lax.fori_loop(0, waves, filter_wave, 0)

    def arrived(ref, w, sem):
        rows = ref.at[:, :, :, pl.ds(w * n_dev, n_dev), :]
        return pltpu.make_async_copy(rows, rows, sem)

    num = den = None

    def rotate(w):
        for i, ref in enumerate((filt_all, appl_all)):
            arrived(ref, w, precv.at[w, i]).wait()
        last = w == waves - 1
        rows = pl.ds(w * n_dev, n_dev)

        def body(t, c):
            p, b = t // BLK, t % BLK
            for h in range(n_sub // 2):
                pair = (2 * h, 2 * h + 1)
                f = jnp.concatenate(
                    [ref[p, b, s, rows, :] for ref in (filt_all, appl_all) for s in pair], axis=1
                )
                hi, lo = split(f)
                out = jnp.dot(
                    est[w], jnp.concatenate([hi, hi, lo], axis=0), preferred_element_type=jnp.float32
                )
                for j, s in enumerate(pair):
                    col = pl.ds(
                        pl.multiple_of((p * n_sub * BLK + s * BLK + b) * LANES, LANES), LANES
                    )
                    x = out[:, j * LANES : (j + 1) * LANES]
                    y = out[:, (2 + j) * LANES : (3 + j) * LANES]
                    if w > 0:
                        x += rot[:, col]
                        y += rota[:, col]
                    rot[:, col] = x
                    rota[:, col] = y
                    if last:
                        c = (c[0] + x * y, c[1] + x * x)
            return c

        zero = jnp.zeros((norb, LANES), jnp.float32)
        return lax.fori_loop(0, n_plane * BLK, body, (zero, zero) if last else 0)

    for w in range(waves):

        def arrival(i, c, w=w):
            g = other_group(i)
            zarrival(w, g).wait_recv()
            process(w, g)
            return c

        lax.fori_loop(0, outer - 1, arrival, 0)
        if w > 0:
            rotate(w - 1)
    num, den = rotate(waves - 1)

    out_rot = pltpu.make_async_copy(rot, rot_hbm, out_sem.at[0])
    out_rot.start()
    quot[...] = jnp.zeros_like(quot)
    quot[0, 0:1, :] = jnp.sum(num.T, axis=0, keepdims=True)
    quot[0, 1:2, :] = jnp.sum(den.T, axis=0, keepdims=True)

    def qcopy(k):
        return pltpu.make_async_remote_copy(
            src_ref=quot.at[0],
            dst_ref=quot_in.at[k],
            send_sem=qsend.at[k],
            recv_sem=qrecv.at[k],
            device_id=device((me + k) % n_dev),
            device_id_type=MESH,
        )

    def qstart(k, c):
        qcopy(k).start()
        return c

    lax.fori_loop(1, n_dev, qstart, 0)

    n_rows = n_plane * BLK

    def gram_body(t, c):
        p, b = t // BLK, t % BLK
        f = jnp.concatenate([filt_all[p, b, s] for s in range(n_sub)], axis=1)
        a = jnp.concatenate([appl_all[p, b, s] for s in range(n_sub)], axis=1)
        fh, fl = split(f)
        ah, al = split(a)
        nt = functools.partial(
            lax.dot_general,
            dimension_numbers=(((1,), (1,)), ((), ())),
            preferred_element_type=jnp.float32,
        )
        high = nt(jnp.concatenate([fh, fl], axis=0), jnp.concatenate([fh, ah], axis=0))
        low = nt(fh, jnp.concatenate([fl, al], axis=0))
        return c + (high[:norb] + (high[norb:] + low))

    both = lax.fori_loop(0, n_rows, gram_body, jnp.zeros((norb, 2 * norb), jnp.float32))
    for w in range(waves):
        rows = both[w * n_dev : (w + 1) * n_dev]
        part[:, w : w + 1, :] = rows[:, None, :norb]
        part[:, waves + w : waves + w + 1, :] = rows[:, None, norb:]

    def gcopy(k):
        to = (me + k) % n_dev
        return pltpu.make_async_remote_copy(
            src_ref=part.at[to],
            dst_ref=part_in.at[k],
            send_sem=gsend.at[k],
            recv_sem=grecv.at[k],
            device_id=device(to),
            device_id_type=MESH,
        )

    def gstart(k, c):
        gcopy(k).start()
        return c

    lax.fori_loop(1, n_dev, gstart, 0)

    def qfinish(k, total):
        qcopy(k).wait()
        return total + quot_in[k]

    total = lax.fori_loop(1, n_dev, qfinish, quot[0]) / npts
    ritz = total[0:1] / (total[1:2] + quot_eps)
    ritz_out[...] = ritz
    column = jnp.broadcast_to(ritz, (LANES, norb)).T

    n_cols = rot.shape[1] // LANES

    def residual(t, c):
        col = pl.ds(pl.multiple_of(t * LANES, LANES), LANES)
        rota[:, col] = rota[:, col] - column * rot[:, col]
        return c

    lax.fori_loop(0, n_cols, residual, 0)
    out_res = pltpu.make_async_copy(rota, res_hbm, out_sem.at[1])
    out_res.start()

    def gfinish(k, total):
        gcopy(k).wait()
        return total + part_in[k]

    sums = lax.fori_loop(1, n_dev, gfinish, part[me]) / npts
    gram_out[...] = sums[:waves]
    hamil_out[...] = sums[waves : 2 * waves]

    for w in range(waves):
        for i in range(outer - 1):
            zcopy(w, i).wait_send()
        share = n_dev * (peers - 1) // peers
        for i, ref in enumerate((filt_all, appl_all)):
            rows = ref.at[:, :, :, pl.ds(0, share), :]
            pltpu.make_async_copy(rows, rows, psend.at[w, i]).wait()
    out_rot.wait()
    out_res.wait()


def on_device(orbitals, potential, cutoff, eigvec):
    norb = eigvec.shape[0]
    n_ob, n_pt = lax.axis_size("ob"), lax.axis_size("pt")
    n_dev, outer = n_ob * n_pt, n_ob // 2
    waves, npts = orbitals.shape
    tiles = npts // LANES
    ppl = G // outer
    rows = tiles // n_dev
    n_plane, n_sub = max(1, rows // ROWS), min(SUBS, rows // BLK)
    orb = orbitals.reshape(waves, tiles, LANES).transpose(1, 0, 2)
    orb = orb.reshape(G, SUBS, BLK * waves, LANES)
    pot = potential.reshape(G, SUBS, BLK, LANES)
    eig = eigvec.reshape(n_dev, waves, norb).transpose(1, 0, 2).reshape(norb, norb)
    f32 = lambda *s: jax.ShapeDtypeStruct(s, jnp.float32)
    vm = lambda *s: pltpu.VMEM(s, jnp.float32)
    dma = pltpu.SemaphoreType.DMA
    vmem = pl.BlockSpec(memory_space=pltpu.VMEM)
    anywhere = pl.BlockSpec(memory_space=pl.ANY)
    padded = -(-2 * waves // SUBS) * SUBS
    gram, hamil, ritz, rotated, residual = pl.pallas_call(
        functools.partial(kernel, n_ob, n_pt),
        out_shape=(
            f32(waves, norb), f32(waves, norb), f32(1, norb),
            f32(norb, rows * LANES), f32(norb, rows * LANES),
        ),
        in_specs=[pl.BlockSpec(memory_space=pltpu.SMEM), anywhere, anywhere, vmem],
        out_specs=(vmem, vmem, vmem, anywhere, anywhere),
        scratch_shapes=[
            vm(waves, G + 2, BLK, SUBS, LANES),
            vm(G, BLK, SUBS, LANES),
            vm(G, BLK, SUBS, LANES),
            vm(G, BLK, SUBS, LANES),
            pltpu.VMEM((2 * LANES, 2 * LANES), jnp.bfloat16),
            vm(outer, waves, ppl + 2, BLK, SUBS, LANES),
            vm(outer, waves, ppl, BLK, SUBS, LANES),
            vm(n_plane, BLK, n_sub, norb, LANES),
            vm(n_plane, BLK, n_sub, norb, LANES),
            pltpu.VMEM((waves, norb, 3 * n_dev), jnp.bfloat16),
            vm(norb, rows * LANES),
            vm(norb, rows * LANES),
            vm(1, SUBS, norb),
            vm(n_dev, SUBS, norb),
            vm(n_dev, padded, norb),
            vm(n_dev, padded, norb),
            dma((waves, BLK)), dma((BLK,)),
            dma((waves, outer)), dma((waves, outer)),
            dma((waves, 2)), dma((waves, 2)),
            dma((n_dev,)), dma((n_dev,)), dma((n_dev,)), dma((n_dev,)),
            dma((2,)),
        ],
        compiler_params=pltpu.CompilerParams(
            collective_id=0, has_side_effects=True, vmem_limit_bytes=60 * 2**20
        ),
        name="filter_rotate",
    )(cutoff, pot, orb, eig)
    back = lambda m: m.reshape(waves, waves, n_dev).transpose(0, 2, 1).reshape(waves, norb)
    return (back(gram), back(hamil), rotated, residual, ritz[0])


def solution(mesh):
    return jax.shard_map(
        on_device,
        mesh=mesh,
        in_specs=(P(("ob", "pt"), None), P(), P(), P()),
        out_specs=(
            P(("ob", "pt"), None),
            P(("ob", "pt"), None),
            P(None, ("ob", "pt")),
            P(None, ("ob", "pt")),
            P(),
        ),
        check_vma=False,
    )
```

```python
import functools

import jax
import jax.numpy as jnp
from jax import lax
from jax.experimental import pallas as pl
from jax.experimental.pallas import tpu as pltpu
from jax.sharding import PartitionSpec as P

G = 64
DEGREE = 12
LANES = 128
SUBS = 8
ROWS = G * G // LANES
BLK = ROWS // SUBS
CHUNK = 16
MESH = pl.DeviceIdType.MESH
upper_bound = 8.0
quot_eps = 1e-06


def split(x):
    hi = x.astype(jnp.bfloat16)
    return hi, (x - hi.astype(jnp.float32)).astype(jnp.bfloat16)


def shift_matrix():
    row = lax.broadcasted_iota(jnp.int32, (2 * LANES, 2 * LANES), 0) % LANES
    col = lax.broadcasted_iota(jnp.int32, (2 * LANES, 2 * LANES), 1)
    lane = col % LANES
    step = (row - lane) % G
    z_pair = (row // G == lane // G) & ((step == 1) | (step == G - 1))
    swap = (row + G) % LANES == lane
    both = jnp.where(swap, 1.0, 0.0) + jnp.where((col < LANES) & z_pair, 1.0, 0.0)
    return both.astype(jnp.bfloat16)


def lateral(v, shifts):
    hi, lo = split(v.reshape(-1, LANES))
    both = jnp.dot(
        jnp.concatenate([hi, lo], axis=1), shifts, preferred_element_type=jnp.float32
    )
    near = both[:, :LANES].reshape(v.shape)
    w = both[:, LANES:].reshape(v.shape)
    below = jnp.concatenate([pltpu.roll(w[:, BLK - 1 :], 1, 2), w[:, : BLK - 1]], axis=1)
    above = jnp.concatenate([w[:, 1:], pltpu.roll(w[:, :1], SUBS - 1, 2)], axis=1)
    low = lax.broadcasted_iota(jnp.int32, (1, 1, 1, LANES), 3) < G
    return near + jnp.where(low, below, above)


def kernel(
    n_ob, n_pt,
    cut_ref, pot_hbm, orb_hbm, eig_hbm,
    gram_out, hamil_out, ritz_out, rot, rota,
    eig, ext, spare, coef, pot, shifts, zbuf, appl, filt_all, appl_all, est,
    quot, quot_in, part, part_in,
    load_sem, pot_sem, eig_sem, zsend, zrecv, psend, precv, qsend, qrecv, gsend, grecv,
):
    waves = ext.shape[0]
    outer, peers, n_dev = n_ob // 2, 2 * n_pt, n_ob * n_pt
    norb = eig.shape[1]
    ppl = G // outer
    n_plane, _, n_sub = filt_all.shape[:3]
    per_plane = SUBS // n_sub
    npts = G * G * G
    ob, pt = lax.axis_index("ob"), lax.axis_index("pt")
    me = ob * n_pt + pt
    group = ob // 2
    seat = ob % 2 * n_pt + pt

    def device(i):
        return (i // n_pt, i % n_pt)

    half = group // max(1, outer // 2)
    mirrored = half * (outer - 1 - group) + (1 - half) * group

    def other_group(i, ends, middles):
        if outer == 4:
            t = ends[i] + mirrored * (middles[i] - ends[i])
        else:
            t = outer - 1 - i - (i + mirrored + 1) // outer
        return half * (outer - 1 - t) + (1 - half) * t

    def target(i):
        return other_group(i, (3, 2, 1), (2, 3, 0))

    def source(i):
        return other_group(i, (3, 1, 2), (3, 0, 2))

    barrier = pltpu.get_barrier_semaphore()

    def greet(k, c):
        pl.semaphore_signal(
            barrier, inc=1, device_id=device((me + k) % n_dev), device_id_type=MESH
        )
        return c

    def load(w, b):
        return pltpu.make_async_copy(
            orb_hbm.at[:, :, b * waves + w, :], ext.at[w, pl.ds(1, G), b], load_sem.at[w, b]
        )

    def load_pot(b):
        return pltpu.make_async_copy(pot_hbm.at[:, :, b, :], pot.at[:, b], pot_sem.at[b])

    def load_eig(w):
        return pltpu.make_async_copy(
            eig_hbm.at[:, w, :], eig.at[pl.ds(w * n_dev, n_dev)], eig_sem.at[w]
        )

    for b in range(BLK):
        load(0, b).start()
    for b in range(BLK):
        load_pot(b).start()
    for w in range(1, waves):
        for b in range(BLK):
            load(w, b).start()
    for w in range(waves):
        load_eig(w).start()
    lax.fori_loop(1, n_dev, greet, 0)

    cut = cut_ref[0]
    center = 0.5 * (upper_bound + cut)
    half_width = 0.5 * (upper_bound - cut)
    inv = 1.0 / half_width
    shifts[...] = shift_matrix()
    for b in range(BLK):
        load_pot(b).wait()

    def prep(x, c):
        coef[x] = (2.0 * inv) * (pot[x] + (3.0 - center))
        return c

    lax.fori_loop(0, G, prep, 0)

    def sweep(cur, dst, first):
        for q in range(G // CHUNK):
            lat = lateral(cur[pl.ds(q * CHUNK, CHUNK)], shifts[...])
            for u in range(CHUNK):
                x = q * CHUNK + u
                s = (cur[(x - 1) % G] + cur[(x + 1) % G]) + lat[u]
                g = coef[x] * cur[x] - inv * s
                dst[x] = 0.5 * g if first else g - dst[x]

    def zcopy(w, i):
        to = target(i)
        return pltpu.make_async_remote_copy(
            src_ref=ext.at[w, pl.ds(to * ppl, ppl + 2)],
            dst_ref=zbuf.at[group, w],
            send_sem=zsend.at[w, to],
            recv_sem=zrecv.at[w, group],
            device_id=(to * 2 + ob % 2, pt),
            device_id_type=MESH,
        )

    def send_wave(w):
        for i in range(outer - 1):
            zcopy(w, i).start()

    def zarrival(w, g):
        return pltpu.make_async_remote_copy(
            src_ref=zbuf.at[g, w],
            dst_ref=zbuf.at[g, w],
            send_sem=zsend.at[w, g],
            recv_sem=zrecv.at[w, g],
            device_id=(g * 2 + ob % 2, pt),
            device_id_type=MESH,
        )

    def piece(ref, first_plane, to):
        planes = pl.ds(first_plane + to // per_plane * n_plane, n_plane)
        if n_sub == SUBS:
            return ref.at[planes]
        return ref.at[planes, :, pl.ds(pl.multiple_of(to % per_plane * n_sub, n_sub), n_sub)]

    def dispatch(w, g, i):
        src, first = ((zbuf, 1), (appl, 0))[i]
        dst = (filt_all, appl_all)[i].at[:, :, :, w * n_dev + g * peers + seat, :]

        def send(k, c):
            to = (seat + k) % peers
            pltpu.make_async_remote_copy(
                src_ref=piece(src.at[g, w], first, to),
                dst_ref=dst,
                send_sem=psend.at[w, i],
                recv_sem=precv.at[w, i],
                device_id=(group * 2 + to // n_pt, to % n_pt),
                device_id_type=MESH,
            ).start()
            return c

        lax.fori_loop(1, peers, send, 0)
        pltpu.make_async_copy(piece(src.at[g, w], first, seat), dst, precv.at[w, i]).start()

    def process(w, g):
        dispatch(w, g, 0)
        src = zbuf.at[g, w]
        lat = lateral(src[pl.ds(1, ppl)], shifts[...])
        for x in range(ppl):
            s = (src[x] + src[x + 2]) + lat[x]
            appl[g, w, x] = (pot[group * ppl + x] + 3.0) * src[x + 1] - 0.5 * s
        dispatch(w, g, 1)

    def filter_wave(w, c):
        for b in range(BLK):
            load(w, b).wait()
        f = ext.at[w, pl.ds(1, G)]
        sweep(f, spare, True)

        def pair(j, c):
            sweep(spare, f, False)
            sweep(f, spare, False)
            return c

        lax.fori_loop(0, (DEGREE - 2) // 2, pair, 0)
        sweep(spare, f, False)
        ext[w, 0] = ext[w, G]
        ext[w, G + 1] = ext[w, 1]

        @pl.when(w == 0)
        def _():
            pl.semaphore_wait(barrier, n_dev - 1)

        @pl.when((w == 0) | (mirrored > 0))
        def _():
            send_wave(w)

        zbuf[group, w] = ext[w, pl.ds(group * ppl, ppl + 2)]
        process(w, group)
        return c

    lax.fori_loop(0, waves, filter_wave, 0)
    for w in range(waves):
        load_eig(w).wait()
        hi, lo = split(eig[pl.ds(w * n_dev, n_dev), :].T)
        est[w] = jnp.concatenate([hi, lo, hi], axis=1)

    def arrived(ref, w, sem):
        rows = ref.at[:, :, :, pl.ds(w * n_dev, n_dev), :]
        return pltpu.make_async_copy(rows, rows, sem)

    num = den = None

    def rotate(w):
        for i, ref in enumerate((filt_all, appl_all)):
            arrived(ref, w, precv.at[w, i]).wait()
        last = w == waves - 1
        rows = pl.ds(w * n_dev, n_dev)

        def body(t, c):
            p, b = t // BLK, t % BLK
            for h in range(n_sub // 2):
                pair = (2 * h, 2 * h + 1)
                f = jnp.concatenate(
                    [ref[p, b, s, rows, :] for ref in (filt_all, appl_all) for s in pair], axis=1
                )
                hi, lo = split(f)
                out = jnp.dot(
                    est[w], jnp.concatenate([hi, hi, lo], axis=0), preferred_element_type=jnp.float32
                )
                for j, s in enumerate(pair):
                    col = pl.ds(
                        pl.multiple_of((p * n_sub * BLK + s * BLK + b) * LANES, LANES), LANES
                    )
                    x = out[:, j * LANES : (j + 1) * LANES]
                    y = out[:, (2 + j) * LANES : (3 + j) * LANES]
                    if w > 0:
                        x += rot[:, col]
                        y += rota[:, col]
                    rot[:, col] = x
                    rota[:, col] = y
                    if last:
                        c = (c[0] + x * y, c[1] + x * x)
            return c

        zero = jnp.zeros((norb, LANES), jnp.float32)
        return lax.fori_loop(0, n_plane * BLK, body, (zero, zero) if last else 0)

    for w in range(waves):

        for i in range(outer - 1):
            with jax.named_scope(f"arr_{w}_{i}"):
                zarrival(w, source(i)).wait_recv()
            if i == outer - 2 and w < waves - 1:
                pl.when(mirrored == 0)(functools.partial(send_wave, w + 1))
            process(w, source(i))
        if w > 0:
            rotate(w - 1)
    num, den = rotate(waves - 1)

    quot[...] = jnp.zeros_like(quot)
    quot[0, 0:1, :] = jnp.sum(num.T, axis=0, keepdims=True)
    quot[0, 1:2, :] = jnp.sum(den.T, axis=0, keepdims=True)

    def qcopy(k):
        return pltpu.make_async_remote_copy(
            src_ref=quot.at[0],
            dst_ref=quot_in.at[k],
            send_sem=qsend.at[k],
            recv_sem=qrecv.at[k],
            device_id=device((me + k) % n_dev),
            device_id_type=MESH,
        )

    def qstart(k, c):
        qcopy(k).start()
        return c

    lax.fori_loop(1, n_dev, qstart, 0)

    n_rows = n_plane * BLK

    def gram_body(t, c):
        p, b = t // BLK, t % BLK
        f = jnp.concatenate([filt_all[p, b, s] for s in range(n_sub)], axis=1)
        a = jnp.concatenate([appl_all[p, b, s] for s in range(n_sub)], axis=1)
        fh, fl = split(f)
        ah, al = split(a)
        nt = functools.partial(
            lax.dot_general,
            dimension_numbers=(((1,), (1,)), ((), ())),
            preferred_element_type=jnp.float32,
        )
        high = nt(jnp.concatenate([fh, fl], axis=0), jnp.concatenate([fh, ah], axis=0))
        low = nt(fh, jnp.concatenate([fl, al], axis=0))
        return c + (high[:norb] + (high[norb:] + low))

    both = lax.fori_loop(0, n_rows, gram_body, jnp.zeros((norb, 2 * norb), jnp.float32))
    for w in range(waves):
        rows = both[w * n_dev : (w + 1) * n_dev]
        part[:, w : w + 1, :] = rows[:, None, :norb]
        part[:, waves + w : waves + w + 1, :] = rows[:, None, norb:]

    def gcopy(k):
        to = (me + k) % n_dev
        return pltpu.make_async_remote_copy(
            src_ref=part.at[to],
            dst_ref=part_in.at[k],
            send_sem=gsend.at[k],
            recv_sem=grecv.at[k],
            device_id=device(to),
            device_id_type=MESH,
        )

    def gstart(k, c):
        gcopy(k).start()
        return c

    lax.fori_loop(1, n_dev, gstart, 0)

    def qfinish(k, total):
        qcopy(k).wait()
        return total + quot_in[k]

    total = lax.fori_loop(1, n_dev, qfinish, quot[0]) / npts
    ritz = total[0:1] / (total[1:2] + quot_eps)
    ritz_out[...] = ritz
    column = jnp.broadcast_to(ritz, (LANES, norb)).T

    width = SUBS * LANES if rot.shape[1] % (SUBS * LANES) == 0 else LANES

    def residual(k, c):
        for t in range(width // LANES):
            col = pl.ds(pl.multiple_of(k * width + t * LANES, LANES), LANES)
            rota[:, col] = rota[:, col] - column * rot[:, col]
        return c

    lax.fori_loop(0, rot.shape[1] // width, residual, 0)

    def gfinish(k, total):
        gcopy(k).wait()
        return total + part_in[k]

    sums = lax.fori_loop(1, n_dev, gfinish, part[me]) / npts
    row = lax.broadcasted_iota(jnp.int32, (norb, norb), 0)
    col = lax.broadcasted_iota(jnp.int32, (norb, norb), 1)
    place = jnp.where(row % n_dev * waves + row // n_dev == col, 1.0, 0.0)
    sums = jnp.dot(
        sums, place, precision=lax.Precision.HIGHEST, preferred_element_type=jnp.float32
    )
    gram_out[...] = sums[:waves]
    hamil_out[...] = sums[waves : 2 * waves]

    for w in range(waves):
        for i in range(outer - 1):
            zcopy(w, i).wait_send()
        share = n_dev * (peers - 1) // peers
        for i, ref in enumerate((filt_all, appl_all)):
            rows = ref.at[:, :, :, pl.ds(0, share), :]
            pltpu.make_async_copy(rows, rows, psend.at[w, i]).wait()


def store_kernel(*refs):
    n = (len(refs) - 1) // 2
    copies = [pltpu.make_async_copy(refs[i], refs[n + i], refs[-1].at[i]) for i in range(n)]
    for copy in copies:
        copy.start()
    for copy in copies:
        copy.wait()


def store(*arrays):
    return pl.pallas_call(
        store_kernel,
        out_shape=tuple(jax.ShapeDtypeStruct(a.shape, a.dtype) for a in arrays),
        in_specs=[pl.BlockSpec(memory_space=pltpu.VMEM)] * len(arrays),
        out_specs=tuple([pl.BlockSpec(memory_space=pl.ANY)] * len(arrays)),
        scratch_shapes=[pltpu.SemaphoreType.DMA((len(arrays),))],
        compiler_params=pltpu.CompilerParams(vmem_limit_bytes=20 * 2**20),
        name="store",
    )(*arrays)


def on_device(orbitals, potential, cutoff, eigvec):
    norb = eigvec.shape[0]
    n_ob, n_pt = lax.axis_size("ob"), lax.axis_size("pt")
    n_dev, outer = n_ob * n_pt, n_ob // 2
    waves, npts = orbitals.shape
    tiles = npts // LANES
    ppl = G // outer
    rows = tiles // n_dev
    n_plane, n_sub = max(1, rows // ROWS), min(SUBS, rows // BLK)
    orb = orbitals.reshape(waves, tiles, LANES).transpose(1, 0, 2)
    orb = orb.reshape(G, SUBS, BLK * waves, LANES)
    pot = potential.reshape(G, SUBS, BLK, LANES)
    eig = eigvec.reshape(n_dev, waves, norb)
    f32 = lambda *s: jax.ShapeDtypeStruct(s, jnp.float32)
    vm = lambda *s: pltpu.VMEM(s, jnp.float32)
    dma = pltpu.SemaphoreType.DMA
    vmem = pl.BlockSpec(memory_space=pltpu.VMEM)
    hbm = pl.BlockSpec(memory_space=pltpu.HBM)
    padded = -(-2 * waves // SUBS) * SUBS
    gram, hamil, ritz, rotated, residual = pl.pallas_call(
        functools.partial(kernel, n_ob, n_pt),
        out_shape=(
            f32(waves, norb), f32(waves, norb), f32(1, norb),
            f32(norb, rows * LANES), f32(norb, rows * LANES),
        ),
        in_specs=[pl.BlockSpec(memory_space=pltpu.SMEM), hbm, hbm, hbm],
        out_specs=(vmem,) * 5,
        scratch_shapes=[
            vm(norb, norb),
            vm(waves, G + 2, BLK, SUBS, LANES),
            vm(G, BLK, SUBS, LANES),
            vm(G, BLK, SUBS, LANES),
            vm(G, BLK, SUBS, LANES),
            pltpu.VMEM((2 * LANES, 2 * LANES), jnp.bfloat16),
            vm(outer, waves, ppl + 2, BLK, SUBS, LANES),
            vm(outer, waves, ppl, BLK, SUBS, LANES),
            vm(n_plane, BLK, n_sub, norb, LANES),
            vm(n_plane, BLK, n_sub, norb, LANES),
            pltpu.VMEM((waves, norb, 3 * n_dev), jnp.bfloat16),
            vm(1, SUBS, norb),
            vm(n_dev, SUBS, norb),
            vm(n_dev, padded, norb),
            vm(n_dev, padded, norb),
            dma((waves, BLK)), dma((BLK,)), dma((waves,)),
            dma((waves, outer)), dma((waves, outer)),
            dma((waves, 2)), dma((waves, 2)),
            dma((n_dev,)), dma((n_dev,)), dma((n_dev,)), dma((n_dev,)),
        ],
        compiler_params=pltpu.CompilerParams(
            collective_id=0, has_side_effects=True, vmem_limit_bytes=44 * 2**20
        ),
        name="filter_rotate",
    )(cutoff, pot, orb, eig)
    gram, hamil, rotated, residual, ritz = store(gram, hamil, rotated, residual, ritz)
    return (gram, hamil, rotated, residual, ritz[0])


def solution(mesh):
    return jax.shard_map(
        on_device,
        mesh=mesh,
        in_specs=(P(("ob", "pt"), None), P(), P(), P()),
        out_specs=(
            P(("ob", "pt"), None),
            P(("ob", "pt"), None),
            P(None, ("ob", "pt")),
            P(None, ("ob", "pt")),
            P(),
        ),
        check_vma=False,
    )
```

```python
import functools

import jax
import jax.numpy as jnp
from jax import lax
from jax.experimental import pallas as pl
from jax.experimental.pallas import tpu as pltpu
from jax.sharding import PartitionSpec as P

G = 64
DEGREE = 12
LANES = 128
SUBS = 8
ROWS = G * G // LANES
BLK = ROWS // SUBS
CHUNK = 16
MESH = pl.DeviceIdType.MESH
upper_bound = 8.0
quot_eps = 1e-06


def split(x):
    hi = x.astype(jnp.bfloat16)
    return hi, (x - hi.astype(jnp.float32)).astype(jnp.bfloat16)


def shift_matrix():
    row = lax.broadcasted_iota(jnp.int32, (2 * LANES, 2 * LANES), 0) % LANES
    col = lax.broadcasted_iota(jnp.int32, (2 * LANES, 2 * LANES), 1)
    lane = col % LANES
    step = (row - lane) % G
    z_pair = (row // G == lane // G) & ((step == 1) | (step == G - 1))
    swap = (row + G) % LANES == lane
    both = jnp.where(swap, 1.0, 0.0) + jnp.where((col < LANES) & z_pair, 1.0, 0.0)
    return both.astype(jnp.bfloat16)


def lateral(v, shifts):
    hi, lo = split(v.reshape(-1, LANES))
    both = jnp.dot(
        jnp.concatenate([hi, lo], axis=1), shifts, preferred_element_type=jnp.float32
    )
    near = both[:, :LANES].reshape(v.shape)
    w = both[:, LANES:].reshape(v.shape)
    below = jnp.concatenate([pltpu.roll(w[:, BLK - 1 :], 1, 2), w[:, : BLK - 1]], axis=1)
    above = jnp.concatenate([w[:, 1:], pltpu.roll(w[:, :1], SUBS - 1, 2)], axis=1)
    low = lax.broadcasted_iota(jnp.int32, (1, 1, 1, LANES), 3) < G
    return near + jnp.where(low, below, above)


def kernel(
    n_ob, n_pt,
    cut_ref, pot_hbm, orb_hbm, eig_hbm,
    gram_out, hamil_out, ritz_out, rot, rota,
    eig, ext, spare, coef, pot, shifts, zbuf, appl, filt_all, appl_all, est,
    quot, quot_in, part, part_in,
    load_sem, pot_sem, eig_sem, zsend, zrecv, psend, precv, qsend, qrecv, gsend, grecv,
):
    waves = ext.shape[0]
    outer, peers, n_dev = n_ob // 2, 2 * n_pt, n_ob * n_pt
    norb = eig.shape[1]
    ppl = G // outer
    n_plane, _, n_sub = filt_all.shape[:3]
    per_plane = SUBS // n_sub
    npts = G * G * G
    ob, pt = lax.axis_index("ob"), lax.axis_index("pt")
    me = ob * n_pt + pt
    group = ob // 2
    seat = ob % 2 * n_pt + pt

    def device(i):
        return (i // n_pt, i % n_pt)

    half = group // max(1, outer // 2)
    mirrored = half * (outer - 1 - group) + (1 - half) * group

    def other_group(i, ends, middles):
        if outer == 4:
            t = ends[i] + mirrored * (middles[i] - ends[i])
        else:
            t = outer - 1 - i - (i + mirrored + 1) // outer
        return half * (outer - 1 - t) + (1 - half) * t

    def target(i):
        return other_group(i, (3, 2, 1), (2, 3, 0))

    def source(i):
        return other_group(i, (3, 1, 2), (3, 0, 2))

    barrier = pltpu.get_barrier_semaphore()

    def greet(k, c):
        pl.semaphore_signal(
            barrier, inc=1, device_id=device((me + k) % n_dev), device_id_type=MESH
        )
        return c

    def load(w, b):
        return pltpu.make_async_copy(
            orb_hbm.at[:, :, b * waves + w, :], ext.at[w, pl.ds(1, G), b], load_sem.at[w, b]
        )

    def load_pot(b):
        return pltpu.make_async_copy(pot_hbm.at[:, :, b, :], pot.at[:, b], pot_sem.at[b])

    def load_eig(w):
        return pltpu.make_async_copy(
            eig_hbm.at[:, w, :], eig.at[pl.ds(w * n_dev, n_dev)], eig_sem.at[w]
        )

    for b in range(BLK):
        load_pot(b).start()
    for b in range(BLK):
        load(0, b).start()
    for w in range(1, waves):
        for b in range(BLK):
            load(w, b).start()
    for w in range(waves):
        load_eig(w).start()
    lax.fori_loop(1, n_dev, greet, 0)

    cut = cut_ref[0]
    center = 0.5 * (upper_bound + cut)
    half_width = 0.5 * (upper_bound - cut)
    inv = 1.0 / half_width
    shifts[...] = shift_matrix()
    for b in range(BLK):
        load_pot(b).wait()

    def prep(x, c):
        coef[x] = (2.0 * inv) * (pot[x] + (3.0 - center))
        return c

    lax.fori_loop(0, G, prep, 0)

    def sweep(cur, dst, first):
        for q in range(G // CHUNK):
            lat = lateral(cur[pl.ds(q * CHUNK, CHUNK)], shifts[...])
            for u in range(CHUNK):
                x = q * CHUNK + u
                s = (cur[(x - 1) % G] + cur[(x + 1) % G]) + lat[u]
                g = coef[x] * cur[x] - inv * s
                dst[x] = 0.5 * g if first else g - dst[x]

    def zcopy(w, i):
        to = target(i)
        return pltpu.make_async_remote_copy(
            src_ref=ext.at[w, pl.ds(to * ppl, ppl + 2)],
            dst_ref=zbuf.at[group, w],
            send_sem=zsend.at[w, to],
            recv_sem=zrecv.at[w, group],
            device_id=(to * 2 + ob % 2, pt),
            device_id_type=MESH,
        )

    def send_wave(w):
        for i in range(outer - 1):
            zcopy(w, i).start()

    def zarrival(w, g):
        return pltpu.make_async_remote_copy(
            src_ref=zbuf.at[g, w],
            dst_ref=zbuf.at[g, w],
            send_sem=zsend.at[w, g],
            recv_sem=zrecv.at[w, g],
            device_id=(g * 2 + ob % 2, pt),
            device_id_type=MESH,
        )

    def piece(ref, first_plane, to):
        planes = pl.ds(first_plane + to // per_plane * n_plane, n_plane)
        if n_sub == SUBS:
            return ref.at[planes]
        return ref.at[planes, :, pl.ds(pl.multiple_of(to % per_plane * n_sub, n_sub), n_sub)]

    def dispatch(w, g, i):
        src, first = ((zbuf, 1), (appl, 0))[i]
        dst = (filt_all, appl_all)[i].at[:, :, :, w * n_dev + g * peers + seat, :]

        def send(k, c):
            to = (seat + k) % peers
            pltpu.make_async_remote_copy(
                src_ref=piece(src.at[g, w], first, to),
                dst_ref=dst,
                send_sem=psend.at[w, i],
                recv_sem=precv.at[w, i],
                device_id=(group * 2 + to // n_pt, to % n_pt),
                device_id_type=MESH,
            ).start()
            return c

        lax.fori_loop(1, peers, send, 0)
        pltpu.make_async_copy(piece(src.at[g, w], first, seat), dst, precv.at[w, i]).start()

    def process(w, g):
        dispatch(w, g, 0)
        src = zbuf.at[g, w]
        lat = lateral(src[pl.ds(1, ppl)], shifts[...])
        for x in range(ppl):
            s = (src[x] + src[x + 2]) + lat[x]
            appl[g, w, x] = (pot[group * ppl + x] + 3.0) * src[x + 1] - 0.5 * s
        dispatch(w, g, 1)

    def filter_wave(w, c):
        for b in range(BLK):
            load(w, b).wait()
        f = ext.at[w, pl.ds(1, G)]
        sweep(f, spare, True)

        def pair(j, c):
            sweep(spare, f, False)
            sweep(f, spare, False)
            return c

        lax.fori_loop(0, (DEGREE - 2) // 2, pair, 0)
        sweep(spare, f, False)
        ext[w, 0] = ext[w, G]
        ext[w, G + 1] = ext[w, 1]

        @pl.when(w == 0)
        def _():
            pl.semaphore_wait(barrier, n_dev - 1)

        @pl.when((w == 0) | (mirrored > 0))
        def _():
            send_wave(w)

        zbuf[group, w] = ext[w, pl.ds(group * ppl, ppl + 2)]
        process(w, group)
        return c

    lax.fori_loop(0, waves, filter_wave, 0)
    for w in range(waves):
        load_eig(w).wait()
        hi, lo = split(eig[pl.ds(w * n_dev, n_dev), :].T)
        est[w] = jnp.concatenate([hi, lo, hi], axis=1)

    def arrived(ref, w, sem):
        rows = ref.at[:, :, :, pl.ds(w * n_dev, n_dev), :]
        return pltpu.make_async_copy(rows, rows, sem)

    def rotate(w, which):
        for i in which:
            arrived((filt_all, appl_all)[i], w, precv.at[w, i]).wait()
        last = w == waves - 1
        rows = pl.ds(w * n_dev, n_dev)

        def body(t, c):
            p, b = t // BLK, t % BLK
            for h in range(n_sub // 2):
                pair = (2 * h, 2 * h + 1)
                f = jnp.concatenate(
                    [(filt_all, appl_all)[i][p, b, s, rows, :] for i in which for s in pair],
                    axis=1,
                )
                hi, lo = split(f)
                out = jnp.dot(
                    est[w], jnp.concatenate([hi, hi, lo], axis=0), preferred_element_type=jnp.float32
                )
                for n, (i, s) in enumerate((i, s) for i in which for s in pair):
                    first = pl.multiple_of((p * n_sub * BLK + s * BLK + b) * LANES, LANES)
                    col = pl.ds(first, LANES)
                    ref = (rot, rota)[i]
                    x = out[:, n * LANES : (n + 1) * LANES]
                    if w > 0:
                        x += ref[:, col]
                    ref[:, col] = x
                    if last:
                        c += x * (x if i == 0 else rot[:, col])
            return c

        zero = jnp.zeros((norb, LANES), jnp.float32)
        return lax.fori_loop(0, n_plane * BLK, body, zero if last else 0)

    for w in range(waves):
        for i in range(outer - 1):
            with jax.named_scope(f"arr_{w}_{i}"):
                zarrival(w, source(i)).wait_recv()
            if i == outer - 2 and w < waves - 1:
                pl.when(mirrored == 0)(functools.partial(send_wave, w + 1))
            process(w, source(i))
        if w > 0:
            rotate(w - 1, (0, 1))
    den = rotate(waves - 1, (0,))
    num = rotate(waves - 1, (1,))

    quot[...] = jnp.zeros_like(quot)
    quot[0, 0:1, :] = jnp.sum(num.T, axis=0, keepdims=True)
    quot[0, 1:2, :] = jnp.sum(den.T, axis=0, keepdims=True)

    def qcopy(k):
        return pltpu.make_async_remote_copy(
            src_ref=quot.at[0],
            dst_ref=quot_in.at[k],
            send_sem=qsend.at[k],
            recv_sem=qrecv.at[k],
            device_id=device((me + k) % n_dev),
            device_id_type=MESH,
        )

    def qstart(k, c):
        qcopy(k).start()
        return c

    lax.fori_loop(1, n_dev, qstart, 0)

    n_rows = n_plane * BLK

    def gram_body(t, c):
        p, b = t // BLK, t % BLK
        f = jnp.concatenate([filt_all[p, b, s] for s in range(n_sub)], axis=1)
        a = jnp.concatenate([appl_all[p, b, s] for s in range(n_sub)], axis=1)
        fh, fl = split(f)
        ah, al = split(a)
        nt = functools.partial(
            lax.dot_general,
            dimension_numbers=(((1,), (1,)), ((), ())),
            preferred_element_type=jnp.float32,
        )
        high = nt(jnp.concatenate([fh, fl], axis=0), jnp.concatenate([fh, ah], axis=0))
        low = nt(fh, jnp.concatenate([fl, al], axis=0))
        return c + (high[:norb] + (high[norb:] + low))

    both = lax.fori_loop(0, n_rows, gram_body, jnp.zeros((norb, 2 * norb), jnp.float32))
    for w in range(waves):
        rows = both[w * n_dev : (w + 1) * n_dev]
        part[:, w : w + 1, :] = rows[:, None, :norb]
        part[:, waves + w : waves + w + 1, :] = rows[:, None, norb:]

    def gcopy(k):
        to = (me + k) % n_dev
        return pltpu.make_async_remote_copy(
            src_ref=part.at[to],
            dst_ref=part_in.at[k],
            send_sem=gsend.at[k],
            recv_sem=grecv.at[k],
            device_id=device(to),
            device_id_type=MESH,
        )

    def gstart(k, c):
        gcopy(k).start()
        return c

    lax.fori_loop(1, n_dev, gstart, 0)

    def qfinish(k, total):
        qcopy(k).wait()
        return total + quot_in[k]

    total = lax.fori_loop(1, n_dev, qfinish, quot[0]) / npts
    ritz = total[0:1] / (total[1:2] + quot_eps)
    ritz_out[...] = ritz
    column = jnp.broadcast_to(ritz, (LANES, norb)).T

    width = SUBS * LANES if rot.shape[1] % (SUBS * LANES) == 0 else LANES

    def residual(k, c):
        for t in range(width // LANES):
            col = pl.ds(pl.multiple_of(k * width + t * LANES, LANES), LANES)
            rota[:, col] = rota[:, col] - column * rot[:, col]
        return c

    lax.fori_loop(0, rot.shape[1] // width, residual, 0)

    def gfinish(k, total):
        gcopy(k).wait()
        return total + part_in[k]

    sums = lax.fori_loop(1, n_dev, gfinish, part[me]) / npts
    row = lax.broadcasted_iota(jnp.int32, (norb, norb), 0)
    col = lax.broadcasted_iota(jnp.int32, (norb, norb), 1)
    place = jnp.where(row % n_dev * waves + row // n_dev == col, 1.0, 0.0)
    sums = jnp.dot(
        sums, place, precision=lax.Precision.HIGHEST, preferred_element_type=jnp.float32
    )
    gram_out[...] = sums[:waves]
    hamil_out[...] = sums[waves : 2 * waves]

    for w in range(waves):
        for i in range(outer - 1):
            zcopy(w, i).wait_send()
        share = n_dev * (peers - 1) // peers
        for i, ref in enumerate((filt_all, appl_all)):
            rows = ref.at[:, :, :, pl.ds(0, share), :]
            pltpu.make_async_copy(rows, rows, psend.at[w, i]).wait()


def store_kernel(*refs):
    n = (len(refs) - 1) // 2
    copies = [pltpu.make_async_copy(refs[i], refs[n + i], refs[-1].at[i]) for i in range(n)]
    for copy in copies:
        copy.start()
    for copy in copies:
        copy.wait()


def store(*arrays):
    return pl.pallas_call(
        store_kernel,
        out_shape=tuple(jax.ShapeDtypeStruct(a.shape, a.dtype) for a in arrays),
        in_specs=[pl.BlockSpec(memory_space=pltpu.VMEM)] * len(arrays),
        out_specs=tuple([pl.BlockSpec(memory_space=pl.ANY)] * len(arrays)),
        scratch_shapes=[pltpu.SemaphoreType.DMA((len(arrays),))],
        compiler_params=pltpu.CompilerParams(vmem_limit_bytes=20 * 2**20),
        name="store",
    )(*arrays)


def on_device(orbitals, potential, cutoff, eigvec):
    norb = eigvec.shape[0]
    n_ob, n_pt = lax.axis_size("ob"), lax.axis_size("pt")
    n_dev, outer = n_ob * n_pt, n_ob // 2
    waves, npts = orbitals.shape
    tiles = npts // LANES
    ppl = G // outer
    rows = tiles // n_dev
    n_plane, n_sub = max(1, rows // ROWS), min(SUBS, rows // BLK)
    orb = orbitals.reshape(waves, tiles, LANES).transpose(1, 0, 2)
    orb = orb.reshape(G, SUBS, BLK * waves, LANES)
    pot = potential.reshape(G, SUBS, BLK, LANES)
    eig = eigvec.reshape(n_dev, waves, norb)
    pot, eig = (pltpu.with_memory_space_constraint(a, pltpu.HBM) for a in (pot, eig))
    f32 = lambda *s: jax.ShapeDtypeStruct(s, jnp.float32)
    vm = lambda *s: pltpu.VMEM(s, jnp.float32)
    dma = pltpu.SemaphoreType.DMA
    vmem = pl.BlockSpec(memory_space=pltpu.VMEM)
    hbm = pl.BlockSpec(memory_space=pltpu.HBM)
    padded = -(-2 * waves // SUBS) * SUBS
    gram, hamil, ritz, rotated, residual = pl.pallas_call(
        functools.partial(kernel, n_ob, n_pt),
        out_shape=(
            f32(waves, norb), f32(waves, norb), f32(1, norb),
            f32(norb, rows * LANES), f32(norb, rows * LANES),
        ),
        in_specs=[pl.BlockSpec(memory_space=pltpu.SMEM), hbm, hbm, hbm],
        out_specs=(vmem,) * 5,
        scratch_shapes=[
            vm(norb, norb),
            vm(waves, G + 2, BLK, SUBS, LANES),
            vm(G, BLK, SUBS, LANES),
            vm(G, BLK, SUBS, LANES),
            vm(G, BLK, SUBS, LANES),
            pltpu.VMEM((2 * LANES, 2 * LANES), jnp.bfloat16),
            vm(outer, waves, ppl + 2, BLK, SUBS, LANES),
            vm(outer, waves, ppl, BLK, SUBS, LANES),
            vm(n_plane, BLK, n_sub, norb, LANES),
            vm(n_plane, BLK, n_sub, norb, LANES),
            pltpu.VMEM((waves, norb, 3 * n_dev), jnp.bfloat16),
            vm(1, SUBS, norb),
            vm(n_dev, SUBS, norb),
            vm(n_dev, padded, norb),
            vm(n_dev, padded, norb),
            dma((waves, BLK)), dma((BLK,)), dma((waves,)),
            dma((waves, outer)), dma((waves, outer)),
            dma((waves, 2)), dma((waves, 2)),
            dma((n_dev,)), dma((n_dev,)), dma((n_dev,)), dma((n_dev,)),
        ],
        compiler_params=pltpu.CompilerParams(
            collective_id=0, has_side_effects=True, vmem_limit_bytes=44 * 2**20
        ),
        name="filter_rotate",
    )(cutoff, pot, orb, eig)
    gram, hamil, rotated, residual, ritz = store(gram, hamil, rotated, residual, ritz)
    return (gram, hamil, rotated, residual, ritz[0])


def solution(mesh):
    return jax.shard_map(
        on_device,
        mesh=mesh,
        in_specs=(P(("ob", "pt"), None), P(), P(), P()),
        out_specs=(
            P(("ob", "pt"), None),
            P(("ob", "pt"), None),
            P(None, ("ob", "pt")),
            P(None, ("ob", "pt")),
            P(),
        ),
        check_vma=False,
    )
```

```python
import functools

import jax
import jax.numpy as jnp
from jax import lax
from jax.experimental import pallas as pl
from jax.experimental.pallas import tpu as pltpu
from jax.sharding import PartitionSpec as P

G = 64
DEGREE = 12
LANES = 128
SUBS = 8
ROWS = G * G // LANES
BLK = ROWS // SUBS
CHUNK = 16
PARTS = 8
MESH = pl.DeviceIdType.MESH
upper_bound = 8.0
quot_eps = 1e-06


def split(x):
    hi = x.astype(jnp.bfloat16)
    return hi, (x - hi.astype(jnp.float32)).astype(jnp.bfloat16)


def shift_matrix():
    row = lax.broadcasted_iota(jnp.int32, (2 * LANES, 2 * LANES), 0) % LANES
    col = lax.broadcasted_iota(jnp.int32, (2 * LANES, 2 * LANES), 1)
    lane = col % LANES
    step = (row - lane) % G
    z_pair = (row // G == lane // G) & ((step == 1) | (step == G - 1))
    swap = (row + G) % LANES == lane
    both = jnp.where(swap, 1.0, 0.0) + jnp.where((col < LANES) & z_pair, 1.0, 0.0)
    return both.astype(jnp.bfloat16)


def lateral(v, shifts):
    hi, lo = split(v.reshape(-1, LANES))
    both = jnp.dot(
        jnp.concatenate([hi, lo], axis=1), shifts, preferred_element_type=jnp.float32
    )
    near = both[:, :LANES].reshape(v.shape)
    w = both[:, LANES:].reshape(v.shape)
    below = jnp.concatenate([pltpu.roll(w[:, BLK - 1 :], 1, 2), w[:, : BLK - 1]], axis=1)
    above = jnp.concatenate([w[:, 1:], pltpu.roll(w[:, :1], SUBS - 1, 2)], axis=1)
    low = lax.broadcasted_iota(jnp.int32, (1, 1, 1, LANES), 3) < G
    return near + jnp.where(low, below, above)


def kernel(
    n_ob, n_pt,
    cut_ref, pot_hbm, orb_hbm, eig_hbm,
    gram_out, hamil_out, ritz_out, rot, rota,
    eig, ext, spare, coef, pot, shifts, zbuf, appl, filt_all, appl_all, est,
    quot, quot_in, part, part_in,
    load_sem, pot_sem, eig_sem, zsend, zrecv, psend, precv, qsend, qrecv, gsend, grecv,
):
    waves = ext.shape[0]
    outer, peers, n_dev = n_ob // 2, 2 * n_pt, n_ob * n_pt
    norb = eig.shape[1]
    ppl = G // outer
    n_plane, _, n_sub = filt_all.shape[:3]
    per_plane = SUBS // n_sub
    npts = G * G * G
    ob, pt = lax.axis_index("ob"), lax.axis_index("pt")
    me = ob * n_pt + pt
    group = ob // 2
    seat = ob % 2 * n_pt + pt

    def device(i):
        return (i // n_pt, i % n_pt)

    half = group // max(1, outer // 2)
    mirrored = half * (outer - 1 - group) + (1 - half) * group

    def other_group(i, ends, middles):
        if outer == 4:
            t = ends[i] + mirrored * (middles[i] - ends[i])
        else:
            t = outer - 1 - i - (i + mirrored + 1) // outer
        return half * (outer - 1 - t) + (1 - half) * t

    def target(i):
        return other_group(i, (3, 2, 1), (2, 3, 0))

    def source(i):
        return other_group(i, (3, 1, 2), (3, 0, 2))

    barrier = pltpu.get_barrier_semaphore()

    def greet(k, c):
        pl.semaphore_signal(
            barrier, inc=1, device_id=device((me + k) % n_dev), device_id_type=MESH
        )
        return c

    def load(w, b):
        return pltpu.make_async_copy(
            orb_hbm.at[:, :, b * waves + w, :], ext.at[w, pl.ds(1, G), b], load_sem.at[w, b]
        )

    def load_pot(b):
        return pltpu.make_async_copy(pot_hbm.at[:, :, b, :], pot.at[:, b], pot_sem.at[b])

    def load_eig(w):
        return pltpu.make_async_copy(
            eig_hbm.at[:, w, :], eig.at[pl.ds(w * n_dev, n_dev)], eig_sem.at[w]
        )

    for b in range(BLK):
        load_pot(b).start()
    for b in range(BLK):
        load(0, b).start()
    for w in range(1, waves):
        for b in range(BLK):
            load(w, b).start()
    for w in range(waves):
        load_eig(w).start()
    lax.fori_loop(1, n_dev, greet, 0)

    cut = cut_ref[0]
    center = 0.5 * (upper_bound + cut)
    half_width = 0.5 * (upper_bound - cut)
    inv = 1.0 / half_width
    shifts[...] = shift_matrix()
    for b in range(BLK):
        load_pot(b).wait()

    def prep(q, c):
        planes = pl.ds(q * CHUNK, CHUNK)
        coef[planes] = (2.0 * inv) * (pot[planes] + (3.0 - center))
        return c

    lax.fori_loop(0, G // CHUNK, prep, 0)

    def sweep(cur, dst, first):
        for q in range(G // CHUNK):
            lat = lateral(cur[pl.ds(q * CHUNK, CHUNK)], shifts[...])
            for u in range(CHUNK):
                x = q * CHUNK + u
                s = (cur[(x - 1) % G] + cur[(x + 1) % G]) + lat[u]
                g = coef[x] * cur[x] - inv * s
                dst[x] = 0.5 * g if first else g - dst[x]

    def zcopy(w, i):
        to = target(i)
        return pltpu.make_async_remote_copy(
            src_ref=ext.at[w, pl.ds(to * ppl, ppl + 2)],
            dst_ref=zbuf.at[group, w],
            send_sem=zsend.at[w, to],
            recv_sem=zrecv.at[w, group],
            device_id=(to * 2 + ob % 2, pt),
            device_id_type=MESH,
        )

    def send_wave(w):
        for i in range(outer - 1):
            zcopy(w, i).start()

    def zarrival(w, g):
        return pltpu.make_async_remote_copy(
            src_ref=zbuf.at[g, w],
            dst_ref=zbuf.at[g, w],
            send_sem=zsend.at[w, g],
            recv_sem=zrecv.at[w, g],
            device_id=(g * 2 + ob % 2, pt),
            device_id_type=MESH,
        )

    def piece(ref, first_plane, to):
        planes = pl.ds(first_plane + to // per_plane * n_plane, n_plane)
        if n_sub == SUBS:
            return ref.at[planes]
        return ref.at[planes, :, pl.ds(pl.multiple_of(to % per_plane * n_sub, n_sub), n_sub)]

    def dispatch(w, g, i):
        src, first = ((zbuf, 1), (appl, 0))[i]
        dst = (filt_all, appl_all)[i].at[:, :, :, w * n_dev + g * peers + seat, :]

        def send(k, c):
            to = (seat + k) % peers
            pltpu.make_async_remote_copy(
                src_ref=piece(src.at[g, w], first, to),
                dst_ref=dst,
                send_sem=psend.at[w, i],
                recv_sem=precv.at[w, i],
                device_id=(group * 2 + to // n_pt, to % n_pt),
                device_id_type=MESH,
            ).start()
            return c

        lax.fori_loop(1, peers, send, 0)
        pltpu.make_async_copy(piece(src.at[g, w], first, seat), dst, precv.at[w, i]).start()

    def process(w, g):
        dispatch(w, g, 0)
        src = zbuf.at[g, w]
        lat = lateral(src[pl.ds(1, ppl)], shifts[...])
        for x in range(ppl):
            s = (src[x] + src[x + 2]) + lat[x]
            appl[g, w, x] = (pot[group * ppl + x] + 3.0) * src[x + 1] - 0.5 * s
        dispatch(w, g, 1)

    def filter_wave(w, c):
        for b in range(BLK):
            load(w, b).wait()
        f = ext.at[w, pl.ds(1, G)]
        sweep(f, spare, True)

        def pair(j, c):
            sweep(spare, f, False)
            sweep(f, spare, False)
            return c

        lax.fori_loop(0, (DEGREE - 2) // 2, pair, 0)
        sweep(spare, f, False)
        ext[w, 0] = ext[w, G]
        ext[w, G + 1] = ext[w, 1]

        @pl.when(w == 0)
        def _():
            pl.semaphore_wait(barrier, n_dev - 1)

        @pl.when((w == 0) | (mirrored > 0))
        def _():
            send_wave(w)

        zbuf[group, w] = ext[w, pl.ds(group * ppl, ppl + 2)]
        process(w, group)
        return c

    lax.fori_loop(0, waves, filter_wave, 0)
    for w in range(waves):
        load_eig(w).wait()
        hi, lo = split(eig[pl.ds(w * n_dev, n_dev), :].T)
        est[w] = jnp.concatenate([hi, lo, hi], axis=1)

    def arrived(ref, w, sem):
        rows = ref.at[:, :, :, pl.ds(w * n_dev, n_dev), :]
        return pltpu.make_async_copy(rows, rows, sem)

    def rotate(w, which):
        for i in which:
            arrived((filt_all, appl_all)[i], w, precv.at[w, i]).wait()
        last = w == waves - 1
        rows = pl.ds(w * n_dev, n_dev)

        def body(t, c):
            p, b = t // BLK, t % BLK
            for h in range(n_sub // 2):
                pair = (2 * h, 2 * h + 1)
                f = jnp.concatenate(
                    [(filt_all, appl_all)[i][p, b, s, rows, :] for i in which for s in pair],
                    axis=1,
                )
                hi, lo = split(f)
                out = jnp.dot(
                    est[w], jnp.concatenate([hi, hi, lo], axis=0), preferred_element_type=jnp.float32
                )
                for n, (i, s) in enumerate((i, s) for i in which for s in pair):
                    first = pl.multiple_of((p * n_sub * BLK + s * BLK + b) * LANES, LANES)
                    col = pl.ds(first, LANES)
                    ref = (rot, rota)[i]
                    x = out[:, n * LANES : (n + 1) * LANES]
                    if w > 0:
                        x += ref[:, col]
                    ref[:, col] = x
                    if last:
                        c += x * (x if i == 0 else rot[:, col])
            return c

        zero = jnp.zeros((norb, LANES), jnp.float32)
        return lax.fori_loop(0, n_plane * BLK, body, zero if last else 0)

    for w in range(waves):
        for i in range(outer - 1):
            with jax.named_scope(f"arr_{w}_{i}"):
                zarrival(w, source(i)).wait_recv()
            if i == outer - 2 and w < waves - 1:
                pl.when(mirrored == 0)(functools.partial(send_wave, w + 1))
            process(w, source(i))
        if w > 0:
            rotate(w - 1, (0, 1))
    den = rotate(waves - 1, (0,))
    quot[...] = jnp.zeros_like(quot)
    quot[0, 1:2, :] = jnp.sum(den.T, axis=0, keepdims=True)
    num = rotate(waves - 1, (1,))

    quot[0, 0:1, :] = jnp.sum(num.T, axis=0, keepdims=True)

    def qcopy(k):
        return pltpu.make_async_remote_copy(
            src_ref=quot.at[0],
            dst_ref=quot_in.at[k],
            send_sem=qsend.at[k],
            recv_sem=qrecv.at[k],
            device_id=device((me + k) % n_dev),
            device_id_type=MESH,
        )

    def qstart(k, c):
        qcopy(k).start()
        return c

    lax.fori_loop(1, n_dev, qstart, 0)

    n_rows = n_plane * BLK

    def gram_body(t, c):
        p, b = t // BLK, t % BLK
        f = jnp.concatenate([filt_all[p, b, s] for s in range(n_sub)], axis=1)
        a = jnp.concatenate([appl_all[p, b, s] for s in range(n_sub)], axis=1)
        fh, fl = split(f)
        ah, al = split(a)
        nt = functools.partial(
            lax.dot_general,
            dimension_numbers=(((1,), (1,)), ((), ())),
            preferred_element_type=jnp.float32,
        )
        high = nt(jnp.concatenate([fh, fl], axis=0), jnp.concatenate([fh, ah], axis=0))
        low = nt(fh, jnp.concatenate([fl, al], axis=0))
        return c + (high[:norb] + (high[norb:] + low))

    both = lax.fori_loop(0, n_rows, gram_body, jnp.zeros((norb, 2 * norb), jnp.float32))
    for w in range(waves):
        rows = both[w * n_dev : (w + 1) * n_dev]
        part[:, w : w + 1, :] = rows[:, None, :norb]
        part[:, waves + w : waves + w + 1, :] = rows[:, None, norb:]

    def gcopy(k):
        to = (me + k) % n_dev
        return pltpu.make_async_remote_copy(
            src_ref=part.at[to],
            dst_ref=part_in.at[k],
            send_sem=gsend.at[k],
            recv_sem=grecv.at[k],
            device_id=device(to),
            device_id_type=MESH,
        )

    def gstart(k, c):
        gcopy(k).start()
        return c

    lax.fori_loop(1, n_dev, gstart, 0)

    def qfinish(k, total):
        qcopy(k).wait()
        return total + quot_in[k]

    total = lax.fori_loop(1, n_dev, qfinish, quot[0]) / npts
    ritz = total[0:1] / (total[1:2] + quot_eps)
    ritz_out[...] = ritz
    column = jnp.broadcast_to(ritz, (LANES, norb)).T

    width = SUBS * LANES if rot.shape[1] % (SUBS * LANES) == 0 else LANES

    def residual(k, c):
        for t in range(width // LANES):
            col = pl.ds(pl.multiple_of(k * width + t * LANES, LANES), LANES)
            rota[:, col] = rota[:, col] - column * rot[:, col]
        return c

    lax.fori_loop(0, rot.shape[1] // width, residual, 0)

    def gfinish(k, total):
        gcopy(k).wait()
        return total + part_in[k]

    sums = lax.fori_loop(1, n_dev, gfinish, part[me]) / npts
    row = lax.broadcasted_iota(jnp.int32, (norb, norb), 0)
    col = lax.broadcasted_iota(jnp.int32, (norb, norb), 1)
    place = jnp.where(row % n_dev * waves + row // n_dev == col, 1.0, 0.0)
    sums = jnp.dot(
        sums, place, precision=lax.Precision.HIGHEST, preferred_element_type=jnp.float32
    )
    gram_out[...] = sums[:waves]
    hamil_out[...] = sums[waves : 2 * waves]

    for w in range(waves):
        for i in range(outer - 1):
            zcopy(w, i).wait_send()
        share = n_dev * (peers - 1) // peers
        for i, ref in enumerate((filt_all, appl_all)):
            rows = ref.at[:, :, :, pl.ds(0, share), :]
            pltpu.make_async_copy(rows, rows, psend.at[w, i]).wait()


def store_kernel(*refs):
    n = (len(refs) - 1) // 2
    copies = []
    for i in range(n):
        rows = refs[i].shape[0]
        step = max(SUBS, rows // PARTS)
        for k, first in enumerate(range(0, rows, step)):
            part = pl.ds(first, min(step, rows - first))
            copies.append(
                pltpu.make_async_copy(
                    refs[i].at[part], refs[n + i].at[part], refs[-1].at[i, k]
                )
            )
    for copy in copies:
        copy.start()
    for copy in copies:
        copy.wait()


def store(*arrays):
    return pl.pallas_call(
        store_kernel,
        out_shape=tuple(jax.ShapeDtypeStruct(a.shape, a.dtype) for a in arrays),
        in_specs=[pl.BlockSpec(memory_space=pltpu.VMEM)] * len(arrays),
        out_specs=tuple([pl.BlockSpec(memory_space=pl.ANY)] * len(arrays)),
        scratch_shapes=[pltpu.SemaphoreType.DMA((len(arrays), PARTS))],
        compiler_params=pltpu.CompilerParams(vmem_limit_bytes=20 * 2**20),
        name="store",
    )(*arrays)


def on_device(orbitals, potential, cutoff, eigvec):
    norb = eigvec.shape[0]
    n_ob, n_pt = lax.axis_size("ob"), lax.axis_size("pt")
    n_dev, outer = n_ob * n_pt, n_ob // 2
    waves, npts = orbitals.shape
    tiles = npts // LANES
    ppl = G // outer
    rows = tiles // n_dev
    n_plane, n_sub = max(1, rows // ROWS), min(SUBS, rows // BLK)
    orb = orbitals.reshape(waves, tiles, LANES).transpose(1, 0, 2)
    orb = orb.reshape(G, SUBS, BLK * waves, LANES)
    pot = potential.reshape(G, SUBS, BLK, LANES)
    eig = eigvec.reshape(n_dev, waves, norb)
    pot, eig = (pltpu.with_memory_space_constraint(a, pltpu.HBM) for a in (pot, eig))
    f32 = lambda *s: jax.ShapeDtypeStruct(s, jnp.float32)
    vm = lambda *s: pltpu.VMEM(s, jnp.float32)
    dma = pltpu.SemaphoreType.DMA
    vmem = pl.BlockSpec(memory_space=pltpu.VMEM)
    hbm = pl.BlockSpec(memory_space=pltpu.HBM)
    padded = -(-2 * waves // SUBS) * SUBS
    gram, hamil, ritz, rotated, residual = pl.pallas_call(
        functools.partial(kernel, n_ob, n_pt),
        out_shape=(
            f32(waves, norb), f32(waves, norb), f32(1, norb),
            f32(norb, rows * LANES), f32(norb, rows * LANES),
        ),
        in_specs=[pl.BlockSpec(memory_space=pltpu.SMEM), hbm, hbm, hbm],
        out_specs=(vmem,) * 5,
        scratch_shapes=[
            vm(norb, norb),
            vm(waves, G + 2, BLK, SUBS, LANES),
            vm(G, BLK, SUBS, LANES),
            vm(G, BLK, SUBS, LANES),
            vm(G, BLK, SUBS, LANES),
            pltpu.VMEM((2 * LANES, 2 * LANES), jnp.bfloat16),
            vm(outer, waves, ppl + 2, BLK, SUBS, LANES),
            vm(outer, waves, ppl, BLK, SUBS, LANES),
            vm(n_plane, BLK, n_sub, norb, LANES),
            vm(n_plane, BLK, n_sub, norb, LANES),
            pltpu.VMEM((waves, norb, 3 * n_dev), jnp.bfloat16),
            vm(1, SUBS, norb),
            vm(n_dev, SUBS, norb),
            vm(n_dev, padded, norb),
            vm(n_dev, padded, norb),
            dma((waves, BLK)), dma((BLK,)), dma((waves,)),
            dma((waves, outer)), dma((waves, outer)),
            dma((waves, 2)), dma((waves, 2)),
            dma((n_dev,)), dma((n_dev,)), dma((n_dev,)), dma((n_dev,)),
        ],
        compiler_params=pltpu.CompilerParams(
            collective_id=0, has_side_effects=True, vmem_limit_bytes=44 * 2**20
        ),
        name="filter_rotate",
    )(cutoff, pot, orb, eig)
    gram, hamil, rotated, residual, ritz = store(gram, hamil, rotated, residual, ritz)
    return (gram, hamil, rotated, residual, ritz[0])


def solution(mesh):
    return jax.shard_map(
        on_device,
        mesh=mesh,
        in_specs=(P(("ob", "pt"), None), P(), P(), P()),
        out_specs=(
            P(("ob", "pt"), None),
            P(("ob", "pt"), None),
            P(None, ("ob", "pt")),
            P(None, ("ob", "pt")),
            P(),
        ),
        check_vma=False,
    )
```
